512 devices in a mesh: owner: 128 (over z, y, core), helper: 4 (over x).
Axes of the slice: x: 4, y: 8, z: 8, core: 2. Of those that a mesh axis runs over, the one named last changes fastest.
Arguments:
- embeddings: bfloat16 [196608, 768], P(('owner', 'helper')), may hold values from -16 to 16
- labels: int32 [196608], P(('owner', 'helper')), may hold values from 0 to 32767, as said below
- row_index: int32 [196608], P(('owner', 'helper')), may hold values from 0 to 196607, each once
Outputs:
- nearest: float32 [196608], P(('owner', 'helper'))
The draws below stay inside these ranges and needn't reach their ends.
Inputs may be any that keep to these rules, and one draw needn't show every extreme that they name: Clusters 64 * k to 64 * k + 63 form cluster group k. The 384 rows of one device carry at most 2 labels of any one group, and in every draw one group receives exactly 2 from every device.
All inputs are finite; a program needn't handle non-finite values.
Results may differ from the reference program's by a relative error of at most 0.00044.
Values may be sent and summed in bfloat16 or wider, within the bound.
No kernel may reach another device: no remote copies, remote signals or barrier semaphores. Data moves between devices by JAX's collectives and lax.ppermute only.
A program may use at most 64 MiB of HBM per device.

```python
import jax
import jax.numpy as jnp
from jax import lax

D = 768
ROW_DEV = 384
CLU_DEV = 64
CAP = 2
ROWS = 196608
CLUSTERS = 32768
N_OWNER = 128
N_HELPER = 4


def layout(key):
    groups = CLUSTERS // CLU_DEV
    hot_group = jax.random.randint(jax.random.fold_in(key, 11), (), 0, groups)

    def one_block(block_key):
        key_slots, key_order, key_within = jax.random.split(block_key, 3)
        chosen = jax.random.permutation(key_slots, (groups - 1) * CAP)[:ROW_DEV - CAP] // CAP
        chosen = chosen + (chosen >= hot_group).astype(jnp.int32)
        target = jnp.concatenate([jnp.full((CAP,), hot_group, jnp.int32), chosen.astype(jnp.int32)])
        target = jax.random.permutation(key_order, target)
        within = jax.random.randint(key_within, (ROW_DEV,), 0, CLU_DEV)
        return target * CLU_DEV + within
    block_keys = jax.random.split(jax.random.fold_in(key, 12), groups)
    return jax.vmap(one_block)(block_keys).reshape(-1).astype(jnp.int32)


def draw_labels(key, part):
    return layout(key)


def draw_embeddings(key, part):
    labels = layout(key)
    key_center, key_noise, key_spread = jax.random.split(jax.random.fold_in(key, 21), 3)
    centers = jax.random.normal(key_center, (CLUSTERS, D), jnp.float32)
    spread = jnp.exp(jax.random.uniform(key_spread, (ROWS, 1), jnp.float32, jnp.log(0.25), jnp.log(2.5)))
    noise = jax.random.normal(key_noise, (ROWS, D), jnp.float32)
    values = centers[labels] + spread * noise
    return jnp.clip(values, -16.0, 16.0).astype(jnp.bfloat16)


def setup_inputs(seed: int = 0) -> dict:
    seeds = jax.random.split(jax.random.key(seed), 4)
    return {
        "embeddings": draw_embeddings(jax.random.fold_in(seeds[3], 71), 0),
        "labels": draw_labels(jax.random.fold_in(seeds[3], 71), 0),
        "row_index": jax.random.permutation(seeds[2], ROWS).astype(jnp.int32),
    }


def normalize(embeddings):
    values = embeddings.astype(jnp.float32)
    scale = lax.rsqrt(lax.optimization_barrier(jnp.mean(values * values, axis=1, keepdims=True)) + 1e-06)
    return (values * scale).astype(jnp.bfloat16)

def reference(embeddings, labels, row_index):
    slot_count = N_OWNER * N_HELPER * CAP
    total = labels.shape[0]
    unit_rows = normalize(embeddings)
    unit_padded = jnp.concatenate([unit_rows, jnp.zeros((1, D), jnp.bfloat16)], axis=0)
    label_padded = jnp.concatenate([labels, jnp.full((1,), -1, jnp.int32)])
    index_padded = jnp.concatenate([row_index, jnp.zeros((1,), jnp.int32)])
    home_group = labels // CLU_DEV

    def one_group(group):
        chosen = jnp.nonzero(home_group == group, size=slot_count, fill_value=total)[0].astype(jnp.int32)
        query = unit_padded[chosen]
        query_label = label_padded[chosen]
        query_index = index_padded[chosen]
        scores = jnp.dot(query, query.T, preferred_element_type=jnp.float32) / D
        keep = (query_label[:, None] == query_label[None, :]) & (query_index[None, :] < query_index[:, None])
        largest = lax.optimization_barrier(jnp.max(jnp.where(keep, scores, -3.0), axis=1))
        return (chosen, jnp.maximum(largest, -1.0))
    chosen_all, largest_all = lax.map(one_group, jnp.arange(N_OWNER * N_HELPER, dtype=jnp.int32))
    result = jnp.zeros((total + 1,), jnp.float32).at[chosen_all.reshape(-1)].set(largest_all.reshape(-1))
    return result[:total]
```

```python
import jax
import jax.numpy as jnp
from jax import lax
from jax.experimental import pallas as pl
from jax.experimental.pallas import tpu as pltpu
from jax.sharding import PartitionSpec as P

CLU_DEV = 64
CAP = 2
LANES = 128
BASE = 64
AXES = ("owner", "helper")


def build_slots(emb_ref, label_ref, index_ref, slots_ref, place_ref):
    rows, features = emb_ref.shape
    values = emb_ref[...].astype(jnp.float32)
    scale = lax.rsqrt(jnp.sum(values * values, axis=1, keepdims=True) / features + 1e-06)
    unit = (values * scale).astype(jnp.bfloat16)

    label = label_ref[...]
    order = index_ref[...]
    group = label // CLU_DEV
    zero = jnp.zeros_like(label)
    table = jnp.concatenate(
        [
            label - group * CLU_DEV,
            order % BASE,
            (order // BASE) % BASE,
            order // (BASE * BASE),
            zero + 1,
            group,
            zero,
            zero,
        ],
        axis=0,
    ).astype(jnp.float32)
    columns = table.T
    group_column = columns[:, 5:6]
    group_row = group.astype(jnp.float32)
    earlier = lax.broadcasted_iota(jnp.int32, (rows, rows), 0) < lax.broadcasted_iota(
        jnp.int32, (rows, rows), 1
    )
    rank = jnp.sum(
        jnp.where((group_column == group_row) & earlier, 1.0, 0.0), axis=0, keepdims=True
    )
    place = group * CAP + rank.astype(jnp.int32)
    place_ref[...] = place

    total = slots_ref.shape[0]
    chosen = jnp.where(
        lax.broadcasted_iota(jnp.int32, (total, rows), 0) == place, 1.0, 0.0
    ).astype(jnp.bfloat16)
    slots_ref[:, :features] = jnp.dot(
        chosen, unit, preferred_element_type=jnp.float32
    ).astype(jnp.bfloat16)
    meta = jnp.concatenate(
        [columns, jnp.zeros((rows, LANES - columns.shape[1]), jnp.float32)], axis=1
    ).astype(jnp.bfloat16)
    slots_ref[:, features:] = jnp.dot(
        chosen, meta, preferred_element_type=jnp.float32
    ).astype(jnp.bfloat16)


def keys_of(label, low, middle, high, filled):
    start = label * float(BASE**3)
    key = start + (high * float(BASE * BASE) + middle * float(BASE) + low)
    return start, jnp.where(filled > 0.5, key, -1.0)


def nearest_earlier(rows_ref, out_ref, wide_ref):
    total = rows_ref.shape[0]
    features = rows_ref.shape[1] - LANES
    keys = rows_ref[:, :features]
    meta = rows_ref[:, features:].astype(jnp.float32)
    flat = meta.T
    _, key_row = keys_of(*(flat[k : k + 1, :] for k in range(5)))
    start_column, key_column = keys_of(*(meta[:, k : k + 1] for k in range(5)))
    step = 256
    for begin in range(0, total, step):
        part = slice(begin, begin + step)
        scores = lax.dot_general(
            rows_ref[part, :features],
            keys,
            (((1,), (1,)), ((), ())),
            preferred_element_type=jnp.float32,
        )
        keep = (key_row >= start_column[part]) & (key_row < key_column[part])
        best = jnp.max(jnp.where(keep, scores, -3.0 * features), axis=1, keepdims=True)
        best = jnp.maximum(best / features, -1.0)
        wide_ref[part, :] = jnp.broadcast_to(best, (step, LANES))
    first = wide_ref[pl.ds(0, total // CAP, stride=CAP), :]
    second = wide_ref[pl.ds(1, total // CAP, stride=CAP), :]
    lane = lax.broadcasted_iota(jnp.int32, first.shape, 1)
    out_ref[...] = jnp.where(lane == 0, first, second)


def pick(returned_ref, place_ref, out_ref):
    count = returned_ref.shape[0]
    rows = place_ref.shape[1]
    place = place_ref[...]
    group = place // CAP
    second = (place - group * CAP) > 0
    value = jnp.where(second, returned_ref[:, 1:2], returned_ref[:, 0:1])
    mine = lax.broadcasted_iota(jnp.int32, (count, rows), 0) == group
    out_ref[...] = jnp.sum(jnp.where(mine, value, 0.0), axis=0, keepdims=True)


def on_device(embeddings, labels, row_index):
    rows, features = embeddings.shape
    devices = lax.axis_size("owner") * lax.axis_size("helper")
    total = devices * CAP
    wide = features + LANES
    slots, place = pl.pallas_call(
        build_slots,
        out_shape=(
            jax.ShapeDtypeStruct((total, wide), jnp.bfloat16),
            jax.ShapeDtypeStruct((1, rows), jnp.int32),
        ),
        name="build_slots",
    )(embeddings, labels.reshape(1, rows), row_index.reshape(1, rows))
    got = lax.all_to_all(
        slots.reshape(devices, CAP, wide), AXES, split_axis=0, concat_axis=0, tiled=True
    )
    nearest = pl.pallas_call(
        nearest_earlier,
        out_shape=jax.ShapeDtypeStruct((devices, LANES), jnp.float32),
        scratch_shapes=[pltpu.VMEM((total, LANES), jnp.float32)],
        name="nearest_earlier",
    )(got.reshape(total, wide))
    returned = lax.all_to_all(
        nearest.reshape(devices, 1, LANES), AXES, split_axis=0, concat_axis=0, tiled=True
    )
    return pl.pallas_call(
        pick,
        out_shape=jax.ShapeDtypeStruct((1, rows), jnp.float32),
        name="pick",
    )(returned.reshape(devices, LANES), place).reshape(rows)


def solution(mesh):
    in_specs = (P(AXES, None), P(AXES), P(AXES))
    return jax.shard_map(
        on_device, mesh=mesh, in_specs=in_specs, out_specs=P(AXES), check_vma=False
    )
```

```python
import jax
import jax.numpy as jnp
from jax import lax
from jax.experimental import pallas as pl
from jax.experimental.pallas import tpu as pltpu
from jax.sharding import PartitionSpec as P

CLU_DEV = 64
CAP = 2
LANES = 128
BASE = 64
AXES = ("owner", "helper")


def build_slots(emb_ref, label_ref, index_ref, slots_ref, place_ref, block_ref, sems):
    rows, features = emb_ref.shape
    blocks, count = block_ref.shape[:2]
    values = emb_ref[...].astype(jnp.float32)
    scale = lax.rsqrt(jnp.sum(values * values, axis=1, keepdims=True) / features + 1e-06)
    unit = (values * scale).astype(jnp.bfloat16)

    label = label_ref[...].reshape(1, rows)
    order = index_ref[...].reshape(1, rows)
    group = label // CLU_DEV
    zero = jnp.zeros_like(label)
    table = jnp.concatenate(
        [
            label - group * CLU_DEV,
            order % BASE,
            (order // BASE) % BASE,
            order // (BASE * BASE),
            zero + 1,
            group,
            zero,
            zero,
        ],
        axis=0,
    ).astype(jnp.float32)
    columns = table.T
    group_column = columns[:, 5:6]
    group_row = group.astype(jnp.float32)
    earlier = lax.broadcasted_iota(jnp.int32, (rows, rows), 0) < lax.broadcasted_iota(
        jnp.int32, (rows, rows), 1
    )
    rank = jnp.sum(
        jnp.where((group_column == group_row) & earlier, 1.0, 0.0), axis=0, keepdims=True
    )
    place = group * CAP + rank.astype(jnp.int32)
    place_ref[...] = place

    total = count * CAP
    chosen = jnp.where(
        lax.broadcasted_iota(jnp.int32, (total, rows), 0) == place, 1.0, 0.0
    ).astype(jnp.bfloat16)
    meta = jnp.concatenate(
        [columns, jnp.zeros((rows, LANES - columns.shape[1]), jnp.float32)], axis=1
    ).astype(jnp.bfloat16)
    copies = []
    for block in range(blocks):
        part = meta if block == blocks - 1 else unit[:, block * LANES : (block + 1) * LANES]
        block_ref[block] = (
            jnp.dot(chosen, part, preferred_element_type=jnp.float32)
            .astype(jnp.bfloat16)
            .reshape(count, CAP, LANES)
        )
        copy = pltpu.make_async_copy(
            block_ref.at[block], slots_ref.at[:, block], sems.at[block]
        )
        copy.start()
        copies.append(copy)
    for copy in copies:
        copy.wait()


def keys_of(label, low, middle, high, filled):
    start = label * float(BASE**3)
    key = start + (high * float(BASE * BASE) + middle * float(BASE) + low)
    return start, jnp.where(filled > 0.5, key, -1.0)


def nearest_earlier(got_ref, out_ref, block_ref, rows_ref, wide_ref, sems):
    blocks, count = block_ref.shape[:2]
    total = count * CAP
    features = (blocks - 1) * LANES
    copies = [
        pltpu.make_async_copy(got_ref.at[:, block], block_ref.at[block], sems.at[block])
        for block in range(blocks)
    ]
    for copy in copies[::-1]:
        copy.start()
    copies[-1].wait()
    meta = block_ref[blocks - 1].reshape(total, LANES).astype(jnp.float32)
    flat = meta.T
    _, key_row = keys_of(*(flat[k : k + 1, :] for k in range(5)))
    start_column, key_column = keys_of(*(meta[:, k : k + 1] for k in range(5)))
    for block in range(blocks - 2, -1, -1):
        copies[block].wait()
        rows_ref[:, block * LANES : (block + 1) * LANES] = block_ref[block].reshape(total, LANES)
    step = 256
    for begin in range(0, total, step):
        part = slice(begin, begin + step)
        scores = lax.dot_general(
            rows_ref[part, :],
            rows_ref[...],
            (((1,), (1,)), ((), ())),
            preferred_element_type=jnp.float32,
        )
        keep = (key_row >= start_column[part]) & (key_row < key_column[part])
        best = jnp.max(jnp.where(keep, scores, -3.0 * features), axis=1, keepdims=True)
        best = jnp.maximum(best / features, -1.0)
        wide_ref[part, :] = jnp.broadcast_to(best, (step, LANES))
    first = wide_ref[pl.ds(0, count, stride=CAP), :]
    second = wide_ref[pl.ds(1, count, stride=CAP), :]
    lane = lax.broadcasted_iota(jnp.int32, first.shape, 1)
    out_ref[...] = jnp.where(lane == 0, first, second)


def pick(returned_ref, place_ref, out_ref):
    count = returned_ref.shape[0]
    rows = place_ref.shape[1]
    place = place_ref[...]
    group = place // CAP
    second = (place - group * CAP) > 0
    value = jnp.where(second, returned_ref[:, 1:2], returned_ref[:, 0:1])
    mine = lax.broadcasted_iota(jnp.int32, (count, rows), 0) == group
    out_ref[...] = jnp.sum(jnp.where(mine, value, 0.0), axis=0)


def on_device(embeddings, labels, row_index):
    rows, features = embeddings.shape
    devices = lax.axis_size("owner") * lax.axis_size("helper")
    total = devices * CAP
    blocks = features // LANES + 1
    anywhere = pl.BlockSpec(memory_space=pl.ANY)
    vmem = pl.BlockSpec(memory_space=pltpu.VMEM)
    slots, place = pl.pallas_call(
        build_slots,
        out_shape=(
            jax.ShapeDtypeStruct((devices, blocks, CAP, LANES), jnp.bfloat16),
            jax.ShapeDtypeStruct((1, rows), jnp.int32),
        ),
        out_specs=(anywhere, vmem),
        scratch_shapes=[
            pltpu.VMEM((blocks, devices, CAP, LANES), jnp.bfloat16),
            pltpu.SemaphoreType.DMA((blocks,)),
        ],
        name="build_slots",
    )(embeddings, labels, row_index)
    got = lax.all_to_all(slots, AXES, split_axis=0, concat_axis=0, tiled=True)
    nearest = pl.pallas_call(
        nearest_earlier,
        out_shape=jax.ShapeDtypeStruct((devices, LANES), jnp.float32),
        in_specs=[anywhere],
        scratch_shapes=[
            pltpu.VMEM((blocks, devices, CAP, LANES), jnp.bfloat16),
            pltpu.VMEM((total, features), jnp.bfloat16),
            pltpu.VMEM((total, LANES), jnp.float32),
            pltpu.SemaphoreType.DMA((blocks,)),
        ],
        name="nearest_earlier",
    )(got)
    returned = lax.all_to_all(
        nearest.reshape(devices, 1, LANES), AXES, split_axis=0, concat_axis=0, tiled=True
    )
    return pl.pallas_call(
        pick, out_shape=jax.ShapeDtypeStruct((rows,), jnp.float32), name="pick"
    )(returned.reshape(devices, LANES), place)


def solution(mesh):
    in_specs = (P(AXES, None), P(AXES), P(AXES))
    return jax.shard_map(
        on_device, mesh=mesh, in_specs=in_specs, out_specs=P(AXES), check_vma=False
    )
```

```python
import functools

import jax
import jax.numpy as jnp
from jax import lax
from jax.experimental import pallas as pl
from jax.experimental.pallas import tpu as pltpu
from jax.sharding import PartitionSpec as P

CLU_DEV = 64
CAP = 2
LANES = 128
BASE = 64
AXES = ("owner", "helper")


def build_slots(
    emb_hbm, label_hbm, index_hbm, slots_ref, place_ref, emb_ref, label_ref, index_ref, sems
):
    rows, features = emb_ref.shape
    count = slots_ref.shape[0]
    copies = [
        pltpu.make_async_copy(label_hbm, label_ref, sems.at[0]),
        pltpu.make_async_copy(index_hbm, index_ref, sems.at[1]),
        pltpu.make_async_copy(emb_hbm, emb_ref, sems.at[2]),
    ]
    for copy in copies:
        copy.start()
    copies[0].wait()
    copies[1].wait()
    label = label_ref[...].reshape(1, rows)
    order = index_ref[...].reshape(1, rows)
    group = label // CLU_DEV
    zero = jnp.zeros_like(label)
    table = jnp.concatenate(
        [
            label - group * CLU_DEV + 1,
            order % BASE,
            (order // BASE) % BASE,
            order // (BASE * BASE),
            group,
            zero,
            zero,
            zero,
        ],
        axis=0,
    ).astype(jnp.float32)
    columns = table.T
    group_column = columns[:, 4:5]
    group_row = group.astype(jnp.float32)
    earlier = lax.broadcasted_iota(jnp.int32, (rows, rows), 0) < lax.broadcasted_iota(
        jnp.int32, (rows, rows), 1
    )
    rank = jnp.sum(
        jnp.where((group_column == group_row) & earlier, 1.0, 0.0), axis=0, keepdims=True
    )
    place = group * CAP + rank.astype(jnp.int32)
    place_ref[...] = place

    total = count * CAP
    chosen = jnp.where(
        lax.broadcasted_iota(jnp.int32, (total, rows), 0) == place, 1.0, 0.0
    ).astype(jnp.bfloat16)
    meta = jnp.concatenate(
        [columns, jnp.zeros((rows, LANES - columns.shape[1]), jnp.float32)], axis=1
    ).astype(jnp.bfloat16)
    copies[2].wait()
    values = emb_ref[...].astype(jnp.float32)
    scale = lax.rsqrt(jnp.sum(values * values, axis=1, keepdims=True) / features + 1e-06)
    unit = (values * scale).astype(jnp.bfloat16)
    for block in range(features // LANES + 1):
        begin = block * LANES
        part = meta if begin == features else unit[:, begin : begin + LANES]
        made = jnp.dot(chosen, part, preferred_element_type=jnp.float32).astype(jnp.bfloat16)
        slots_ref[:, block] = made.reshape(count, CAP, LANES)


def digit_weights(shape, axis, span):
    digit = lax.broadcasted_iota(jnp.int32, shape, axis)
    start = jnp.where(digit == 0, float(span), 0.0)
    within = jnp.where(digit == 1, 1.0, jnp.where(digit == 2, float(BASE), 0.0))
    key = start + jnp.where(digit == 3, float(BASE * BASE), within)
    return start.astype(jnp.bfloat16), key.astype(jnp.bfloat16)


def nearest_earlier(span, got_ref, out_ref, rows_ref, wide_ref):
    count, blocks = got_ref.shape[:2]
    total = count * CAP
    features = (blocks - 1) * LANES
    meta = got_ref[:, blocks - 1].reshape(total, LANES)
    start_weights, key_weights = digit_weights((LANES, LANES), 0, span)
    start_column = jnp.dot(meta, start_weights, preferred_element_type=jnp.float32)
    key_column = jnp.dot(meta, key_weights, preferred_element_type=jnp.float32)
    key_row = lax.dot_general(
        digit_weights((8, LANES), 1, span)[1],
        meta,
        (((1,), (1,)), ((), ())),
        preferred_element_type=jnp.float32,
    )[:1, :]
    for block in range(blocks - 1):
        rows_ref[:, block * LANES : (block + 1) * LANES] = got_ref[:, block].reshape(total, LANES)
    step = 256
    for begin in range(0, total, step):
        part = slice(begin, begin + step)
        scores = lax.dot_general(
            rows_ref[part, :],
            rows_ref[...],
            (((1,), (1,)), ((), ())),
            preferred_element_type=jnp.float32,
        )
        best = jnp.full((step, LANES), -3.0 * features, jnp.float32)
        for column in range(0, total, LANES):
            here = key_row[:, column : column + LANES]
            keep = (here >= start_column[part]) & (here < key_column[part])
            best = jnp.where(keep, jnp.maximum(best, scores[:, column : column + LANES]), best)
        best = jnp.max(best, axis=1, keepdims=True)
        best = jnp.maximum(best / features, -1.0)
        wide_ref[part, :] = jnp.broadcast_to(best, (step, LANES))
    first = wide_ref[pl.ds(0, count, stride=CAP), :]
    second = wide_ref[pl.ds(1, count, stride=CAP), :]
    lane = lax.broadcasted_iota(jnp.int32, first.shape, 1)
    out_ref[...] = jnp.where(lane == 0, first, second)


def pick(returned_ref, place_ref, out_ref):
    count = returned_ref.shape[0]
    rows = place_ref.shape[1]
    place = place_ref[...]
    group = place // CAP
    second = (place - group * CAP) > 0
    value = jnp.where(second, returned_ref[:, 1:2], returned_ref[:, 0:1])
    mine = lax.broadcasted_iota(jnp.int32, (count, rows), 0) == group
    out_ref[...] = jnp.sum(jnp.where(mine, value, 0.0), axis=0)


def on_device(embeddings, labels, row_index):
    rows, features = embeddings.shape
    devices = lax.axis_size("owner") * lax.axis_size("helper")
    total = devices * CAP
    blocks = features // LANES + 1
    params = pltpu.CompilerParams(vmem_limit_bytes=24 * 2**20)
    hbm = pl.BlockSpec(memory_space=pltpu.HBM)
    slots, place = pl.pallas_call(
        build_slots,
        out_shape=(
            jax.ShapeDtypeStruct((devices, blocks, CAP, LANES), jnp.bfloat16),
            jax.ShapeDtypeStruct((1, rows), jnp.int32),
        ),
        in_specs=[hbm, hbm, hbm],
        scratch_shapes=[
            pltpu.VMEM((rows, features), jnp.bfloat16),
            pltpu.VMEM((rows,), jnp.int32),
            pltpu.VMEM((rows,), jnp.int32),
            pltpu.SemaphoreType.DMA((3,)),
        ],
        compiler_params=params,
        name="build_slots",
    )(*(pltpu.with_memory_space_constraint(x, pltpu.HBM) for x in (embeddings, labels, row_index)))
    got = lax.all_to_all(slots, AXES, split_axis=0, concat_axis=0, tiled=True)
    nearest = pl.pallas_call(
        functools.partial(nearest_earlier, rows * devices),
        out_shape=jax.ShapeDtypeStruct((devices, LANES), jnp.float32),
        scratch_shapes=[
            pltpu.VMEM((total, features), jnp.bfloat16),
            pltpu.VMEM((total, LANES), jnp.float32),
        ],
        compiler_params=params,
        name="nearest_earlier",
    )(got)
    returned = lax.all_to_all(
        nearest.reshape(devices, 1, LANES), AXES, split_axis=0, concat_axis=0, tiled=True
    )
    return pl.pallas_call(
        pick,
        out_shape=jax.ShapeDtypeStruct((rows,), jnp.float32),
        compiler_params=params,
        name="pick",
    )(returned.reshape(devices, LANES), place)


def solution(mesh):
    in_specs = (P(AXES, None), P(AXES), P(AXES))
    return jax.shard_map(
        on_device, mesh=mesh, in_specs=in_specs, out_specs=P(AXES), check_vma=False
    )
```

```python
import functools

import jax
import jax.numpy as jnp
from jax import lax
from jax.experimental import pallas as pl
from jax.experimental.pallas import tpu as pltpu
from jax.sharding import PartitionSpec as P

CLU_DEV = 64
CAP = 2
LANES = 128
BASE = 64
AXES = ("owner", "helper")


def build_slots(
    emb_hbm, label_hbm, index_hbm, slots_ref, place_ref, emb_ref, label_ref, index_ref, sems
):
    rows, features = emb_ref.shape
    count = slots_ref.shape[0]
    copies = [
        pltpu.make_async_copy(label_hbm, label_ref, sems.at[0]),
        pltpu.make_async_copy(index_hbm, index_ref, sems.at[1]),
        pltpu.make_async_copy(emb_hbm, emb_ref, sems.at[2]),
    ]
    for copy in copies:
        copy.start()
    copies[0].wait()
    copies[1].wait()
    label = label_ref[...].reshape(1, rows)
    order = index_ref[...].reshape(1, rows)
    group = label // CLU_DEV
    zero = jnp.zeros_like(label)
    table = jnp.concatenate(
        [
            label - group * CLU_DEV + 1,
            order % BASE,
            (order // BASE) % BASE,
            order // (BASE * BASE),
            group,
            zero,
            zero,
            zero,
        ],
        axis=0,
    ).astype(jnp.float32)
    columns = table.T
    group_column = columns[:, 4:5]
    group_row = group.astype(jnp.float32)
    earlier = lax.broadcasted_iota(jnp.int32, (rows, rows), 0) < lax.broadcasted_iota(
        jnp.int32, (rows, rows), 1
    )
    rank = jnp.sum(
        jnp.where((group_column == group_row) & earlier, 1.0, 0.0), axis=0, keepdims=True
    )
    place = group * CAP + rank.astype(jnp.int32)
    place_ref[...] = place

    total = count * CAP
    chosen = jnp.where(
        lax.broadcasted_iota(jnp.int32, (total, rows), 0) == place, 1.0, 0.0
    ).astype(jnp.bfloat16)
    meta = jnp.concatenate(
        [columns, jnp.zeros((rows, LANES - columns.shape[1]), jnp.float32)], axis=1
    ).astype(jnp.bfloat16)
    copies[2].wait()
    values = emb_ref[...].astype(jnp.float32)
    scale = lax.rsqrt(jnp.sum(values * values, axis=1, keepdims=True) / features + 1e-06)
    unit = (values * scale).astype(jnp.bfloat16)
    wide = 2 * LANES
    for begin in range(0, features + LANES, wide):
        part = meta if begin == features else unit[:, begin : begin + wide]
        made = jnp.dot(chosen, part, preferred_element_type=jnp.float32)
        made = made.astype(jnp.bfloat16)
        for offset in range(0, part.shape[1], LANES):
            slots_ref[:, (begin + offset) // LANES] = made[:, offset : offset + LANES].reshape(
                count, CAP, LANES
            )


def digit_weights(shape, axis, span):
    digit = lax.broadcasted_iota(jnp.int32, shape, axis)
    start = jnp.where(digit == 0, float(span), 0.0)
    within = jnp.where(digit == 1, 1.0, jnp.where(digit == 2, float(BASE), 0.0))
    key = start + jnp.where(digit == 3, float(BASE * BASE), within)
    return start.astype(jnp.bfloat16), key.astype(jnp.bfloat16)


def nearest_earlier(span, got_ref, out_ref, rows_ref, best_ref):
    count, blocks = got_ref.shape[:2]
    total = count * CAP
    features = (blocks - 1) * LANES
    step = 512
    none = -3.0 * features
    meta = got_ref[:, blocks - 1].reshape(total, LANES)
    column_weights = digit_weights((LANES, LANES), 0, span)
    row_weights = digit_weights((8, LANES), 1, span)
    start_column, key_column = (
        jnp.dot(meta, weights, preferred_element_type=jnp.float32) for weights in column_weights
    )
    start_row, key_row = (
        lax.dot_general(
            weights, meta, (((1,), (1,)), ((), ())), preferred_element_type=jnp.float32
        )[:1, :]
        for weights in row_weights
    )
    crossed = []
    for begin in range(0, total, step):
        here = slice(begin, begin + step)
        for block in range(blocks - 1):
            rows_ref[here, block * LANES : (block + 1) * LANES] = got_ref[
                begin // CAP : (begin + step) // CAP, block
            ].reshape(step, LANES)
        column_best = jnp.full((8, step), none, jnp.float32)
        for other in range(0, begin + step, step):
            part = slice(other, other + step)
            scores = lax.dot_general(
                rows_ref[part, :],
                rows_ref[here, :],
                (((1,), (1,)), ((), ())),
                preferred_element_type=jnp.float32,
            )
            if other < begin:
                best = best_ref[part, :]
            else:
                best = jnp.full((step, LANES), none, jnp.float32)
            for lane in range(0, step, LANES):
                keys = key_row[:, begin + lane : begin + lane + LANES]
                keep = (keys >= start_column[part]) & (keys < key_column[part])
                best = jnp.where(keep, jnp.maximum(best, scores[:, lane : lane + LANES]), best)
            best_ref[part, :] = best
            if other < begin:
                keys = jnp.concatenate([key_column[part]] * (step // LANES), axis=1)
                keep = (keys >= start_row[:, here]) & (keys < key_row[:, here])
                kept = jnp.where(keep, scores, none)
                column_best = jnp.maximum(
                    column_best, jnp.max(kept.reshape(step // 8, 8, step), axis=0)
                )
        crossed.append(column_best)
    for begin in range(0, total, step):
        part = slice(begin, begin + step)
        best = best_ref[part, :]
        if begin:
            best = jnp.maximum(
                best, jnp.concatenate([crossed[begin // step]] * (LANES // 8), axis=0).T
            )
        best = jnp.max(best, axis=1, keepdims=True)
        best = jnp.maximum(best / features, -1.0)
        best_ref[part, :] = jnp.broadcast_to(best, (step, LANES))
    first = best_ref[pl.ds(0, count, stride=CAP), :]
    second = best_ref[pl.ds(1, count, stride=CAP), :]
    lane = lax.broadcasted_iota(jnp.int32, first.shape, 1)
    out_ref[...] = jnp.where(lane == 0, first, second)


def pick(returned_ref, place_ref, out_ref):
    count = returned_ref.shape[0]
    rows = place_ref.shape[1]
    place = place_ref[...]
    group = place // CAP
    second = (place - group * CAP) > 0
    value = jnp.where(second, returned_ref[:, 1:2], returned_ref[:, 0:1])
    mine = lax.broadcasted_iota(jnp.int32, (count, rows), 0) == group
    out_ref[...] = jnp.sum(jnp.where(mine, value, 0.0), axis=0)


def on_device(embeddings, labels, row_index):
    rows, features = embeddings.shape
    devices = lax.axis_size("owner") * lax.axis_size("helper")
    total = devices * CAP
    blocks = features // LANES + 1
    params = pltpu.CompilerParams(vmem_limit_bytes=24 * 2**20)
    hbm = pl.BlockSpec(memory_space=pltpu.HBM)
    slots, place = pl.pallas_call(
        build_slots,
        out_shape=(
            jax.ShapeDtypeStruct((devices, blocks, CAP, LANES), jnp.bfloat16),
            jax.ShapeDtypeStruct((1, rows), jnp.int32),
        ),
        in_specs=[hbm, hbm, hbm],
        scratch_shapes=[
            pltpu.VMEM((rows, features), jnp.bfloat16),
            pltpu.VMEM((rows,), jnp.int32),
            pltpu.VMEM((rows,), jnp.int32),
            pltpu.SemaphoreType.DMA((3,)),
        ],
        compiler_params=params,
        name="build_slots",
    )(*(pltpu.with_memory_space_constraint(x, pltpu.HBM) for x in (embeddings, labels, row_index)))
    got = lax.all_to_all(slots, AXES, split_axis=0, concat_axis=0, tiled=True)
    nearest = pl.pallas_call(
        functools.partial(nearest_earlier, rows * devices),
        out_shape=jax.ShapeDtypeStruct((devices, LANES), jnp.float32),
        scratch_shapes=[
            pltpu.VMEM((total, features), jnp.bfloat16),
            pltpu.VMEM((total, LANES), jnp.float32),
        ],
        compiler_params=params,
        name="nearest_earlier",
    )(got)
    returned = lax.all_to_all(
        nearest.reshape(devices, 1, LANES), AXES, split_axis=0, concat_axis=0, tiled=True
    )
    return pl.pallas_call(
        pick,
        out_shape=jax.ShapeDtypeStruct((rows,), jnp.float32),
        compiler_params=params,
        name="pick",
    )(returned.reshape(devices, LANES), place)


def solution(mesh):
    in_specs = (P(AXES, None), P(AXES), P(AXES))
    return jax.shard_map(
        on_device, mesh=mesh, in_specs=in_specs, out_specs=P(AXES), check_vma=False
    )
```

```python
import functools

import jax
import jax.numpy as jnp
from jax import lax
from jax.experimental import pallas as pl
from jax.experimental.pallas import tpu as pltpu
from jax.sharding import PartitionSpec as P

CLU_DEV = 64
CAP = 2
LANES = 128
BASE = 64
CORES = 2
PEERS = ("ring", "helper")
ALL = ("ring", "helper", "core")


def build_slots(
    helpers, emb_hbm, label_hbm, index_hbm, slots_ref, place_ref, emb_ref, label_ref, index_ref, sems
):
    rows, features = emb_ref.shape
    count = slots_ref.shape[0]
    copies = [
        pltpu.make_async_copy(label_hbm, label_ref, sems.at[0]),
        pltpu.make_async_copy(index_hbm, index_ref, sems.at[1]),
        pltpu.make_async_copy(emb_hbm, emb_ref, sems.at[2]),
    ]
    for copy in copies:
        copy.start()
    copies[0].wait()
    copies[1].wait()
    label = label_ref[...].reshape(1, rows)
    order = index_ref[...].reshape(1, rows)
    group = label // CLU_DEV
    zero = jnp.zeros_like(label)
    table = jnp.concatenate(
        [
            label - group * CLU_DEV + 1,
            order % BASE,
            (order // BASE) % BASE,
            order // (BASE * BASE),
            group,
            zero,
            zero,
            zero,
        ],
        axis=0,
    ).astype(jnp.float32)
    columns = table.T
    group_column = columns[:, 4:5]
    group_row = group.astype(jnp.float32)
    earlier = lax.broadcasted_iota(jnp.int32, (rows, rows), 0) < lax.broadcasted_iota(
        jnp.int32, (rows, rows), 1
    )
    rank = jnp.sum(
        jnp.where((group_column == group_row) & earlier, 1.0, 0.0), axis=0, keepdims=True
    )
    owner = group // helpers
    chip = (owner // CORES) * helpers + group % helpers
    place = (chip * CORES + owner % CORES) * CAP + rank.astype(jnp.int32)
    place_ref[...] = place

    total = count * CAP
    chosen = jnp.where(
        lax.broadcasted_iota(jnp.int32, (total, rows), 0) == place, 1.0, 0.0
    ).astype(jnp.bfloat16)
    meta = jnp.concatenate(
        [columns, jnp.zeros((rows, LANES - columns.shape[1]), jnp.float32)], axis=1
    ).astype(jnp.bfloat16)
    copies[2].wait()
    values = emb_ref[...].astype(jnp.float32)
    scale = lax.rsqrt(jnp.sum(values * values, axis=1, keepdims=True) / features + 1e-06)
    unit = (values * scale).astype(jnp.bfloat16)
    wide = 2 * LANES
    for begin in range(0, features + LANES, wide):
        part = meta if begin == features else unit[:, begin : begin + wide]
        made = jnp.dot(chosen, part, preferred_element_type=jnp.float32)
        made = made.astype(jnp.bfloat16)
        for offset in range(0, part.shape[1], LANES):
            slots_ref[:, (begin + offset) // LANES] = made[:, offset : offset + LANES].reshape(
                count, CAP, LANES
            )


def digit_weights(shape, axis, span):
    digit = lax.broadcasted_iota(jnp.int32, shape, axis)
    start = jnp.where(digit == 0, float(span), 0.0)
    within = jnp.where(digit == 1, 1.0, jnp.where(digit == 2, float(BASE), 0.0))
    key = start + jnp.where(digit == 3, float(BASE * BASE), within)
    return start.astype(jnp.bfloat16), key.astype(jnp.bfloat16)


def nearest_earlier(span, got_ref, out_ref, rows_ref, best_ref):
    count, blocks = got_ref.shape[:2]
    total = count * CAP
    features = (blocks - 1) * LANES
    step = 512
    none = -3.0 * features
    meta = got_ref[:, blocks - 1].reshape(total, LANES)
    column_weights = digit_weights((LANES, LANES), 0, span)
    row_weights = digit_weights((8, LANES), 1, span)
    start_column, key_column = (
        jnp.dot(meta, weights, preferred_element_type=jnp.float32) for weights in column_weights
    )
    start_row, key_row = (
        lax.dot_general(
            weights, meta, (((1,), (1,)), ((), ())), preferred_element_type=jnp.float32
        )[:1, :]
        for weights in row_weights
    )
    crossed = []
    for begin in range(0, total, step):
        here = slice(begin, begin + step)
        for block in range(blocks - 1):
            rows_ref[here, block * LANES : (block + 1) * LANES] = got_ref[
                begin // CAP : (begin + step) // CAP, block
            ].reshape(step, LANES)
        column_best = jnp.full((8, step), none, jnp.float32)
        for other in range(0, begin + step, step):
            part = slice(other, other + step)
            scores = lax.dot_general(
                rows_ref[part, :],
                rows_ref[here, :],
                (((1,), (1,)), ((), ())),
                preferred_element_type=jnp.float32,
            )
            if other < begin:
                best = best_ref[part, :]
            else:
                best = jnp.full((step, LANES), none, jnp.float32)
            for lane in range(0, step, LANES):
                keys = key_row[:, begin + lane : begin + lane + LANES]
                keep = (keys >= start_column[part]) & (keys < key_column[part])
                best = jnp.where(keep, jnp.maximum(best, scores[:, lane : lane + LANES]), best)
            best_ref[part, :] = best
            if other < begin:
                keys = jnp.concatenate([key_column[part]] * (step // LANES), axis=1)
                keep = (keys >= start_row[:, here]) & (keys < key_row[:, here])
                kept = jnp.where(keep, scores, none)
                column_best = jnp.maximum(
                    column_best, jnp.max(kept.reshape(step // 8, 8, step), axis=0)
                )
        crossed.append(column_best)
    for begin in range(0, total, step):
        part = slice(begin, begin + step)
        best = best_ref[part, :]
        if begin:
            best = jnp.maximum(
                best, jnp.concatenate([crossed[begin // step]] * (LANES // 8), axis=0).T
            )
        best = jnp.max(best, axis=1, keepdims=True)
        best = jnp.maximum(best / features, -1.0)
        best_ref[part, :] = jnp.broadcast_to(best, (step, LANES))
    chips = out_ref.shape[0]
    width = CORES * CAP
    lane = lax.broadcasted_iota(jnp.int32, out_ref.shape, 1)
    result = best_ref[pl.ds(0, chips, stride=width), :]
    for k in range(1, width):
        result = jnp.where(lane == k, best_ref[pl.ds(k, chips, stride=width), :], result)
    out_ref[...] = result


def pick(core_ref, same_ref, cross_ref, place_ref, out_ref):
    chips = same_ref.shape[0]
    rows = place_ref.shape[1]
    core = core_ref[0]
    place = place_ref[...]
    chip = place // (CORES * CAP)
    slot = place % CAP
    same = (place // CAP) % CORES == core
    mine = lax.broadcasted_iota(jnp.int32, (chips, rows), 0) == chip

    def column(ref, k):
        return jnp.where(core == 0, ref[:, k : k + 1], ref[:, CAP + k : CAP + k + 1])

    first = jnp.where(same, column(same_ref, 0), column(cross_ref, 0))
    second = jnp.where(same, column(same_ref, 1), column(cross_ref, 1))
    value = jnp.where(slot == 0, first, second)
    out_ref[...] = jnp.sum(jnp.where(mine, value, 0.0), axis=0)


def on_device(embeddings, labels, row_index):
    rows, features = embeddings.shape
    helpers = lax.axis_size("helper")
    chips = lax.axis_size("ring") * helpers
    devices = chips * CORES
    total = devices * CAP
    blocks = features // LANES + 1
    params = pltpu.CompilerParams(vmem_limit_bytes=24 * 2**20)
    hbm = pl.BlockSpec(memory_space=pltpu.HBM)
    slots, place = pl.pallas_call(
        functools.partial(build_slots, helpers),
        out_shape=(
            jax.ShapeDtypeStruct((devices, blocks, CAP, LANES), jnp.bfloat16),
            jax.ShapeDtypeStruct((1, rows), jnp.int32),
        ),
        in_specs=[hbm, hbm, hbm],
        scratch_shapes=[
            pltpu.VMEM((rows, features), jnp.bfloat16),
            pltpu.VMEM((rows,), jnp.int32),
            pltpu.VMEM((rows,), jnp.int32),
            pltpu.SemaphoreType.DMA((3,)),
        ],
        compiler_params=params,
        name="build_slots",
    )(*(pltpu.with_memory_space_constraint(x, pltpu.HBM) for x in (embeddings, labels, row_index)))
    got = lax.all_to_all(slots, ALL, split_axis=0, concat_axis=0, tiled=True)
    nearest = pl.pallas_call(
        functools.partial(nearest_earlier, rows * devices),
        out_shape=jax.ShapeDtypeStruct((chips, LANES), jnp.float32),
        scratch_shapes=[
            pltpu.VMEM((total, features), jnp.bfloat16),
            pltpu.VMEM((total, LANES), jnp.float32),
        ],
        compiler_params=params,
        name="nearest_earlier",
    )(got)
    returned = lax.all_to_all(
        nearest.reshape(chips, 1, LANES), PEERS, split_axis=0, concat_axis=0, tiled=True
    ).reshape(chips, LANES)
    crossed = lax.ppermute(returned, "core", [(k, CORES - 1 - k) for k in range(CORES)])
    vmem = pl.BlockSpec(memory_space=pltpu.VMEM)
    return pl.pallas_call(
        pick,
        out_shape=jax.ShapeDtypeStruct((rows,), jnp.float32),
        in_specs=[pl.BlockSpec(memory_space=pltpu.SMEM), vmem, vmem, vmem],
        compiler_params=params,
        name="pick",
    )(lax.axis_index("core").astype(jnp.int32).reshape(1), returned, crossed, place)


def solution(mesh):
    owners, helpers = mesh.devices.shape
    chips = jax.sharding.Mesh(
        mesh.devices.reshape(owners // CORES, CORES, helpers), ("ring", "core", "helper")
    )
    split = ("ring", "core", "helper")
    return jax.shard_map(
        on_device,
        mesh=chips,
        in_specs=(P(split, None), P(split), P(split)),
        out_specs=P(split),
        check_vma=False,
    )
```

```python
import functools

import jax
import jax.numpy as jnp
from jax import lax
from jax.experimental import pallas as pl
from jax.experimental.pallas import tpu as pltpu
from jax.sharding import PartitionSpec as P

CLU_DEV = 64
CAP = 2
LANES = 128
BASE = 64
CORES = 2
PEERS = ("helper", "ring")
ALL = ("ring", "core", "helper")


def build_slots(
    emb_hbm, label_hbm, index_hbm, slots_ref, place_ref, emb_ref, label_ref, index_ref, sems
):
    rows, features = emb_ref.shape
    count = slots_ref.shape[0]
    copies = [
        pltpu.make_async_copy(label_hbm, label_ref, sems.at[0]),
        pltpu.make_async_copy(index_hbm, index_ref, sems.at[1]),
        pltpu.make_async_copy(emb_hbm, emb_ref, sems.at[2]),
    ]
    for copy in copies:
        copy.start()
    copies[0].wait()
    copies[1].wait()
    label = label_ref[...].reshape(1, rows)
    order = index_ref[...].reshape(1, rows)
    group = label // CLU_DEV
    zero = jnp.zeros_like(label)
    table = jnp.concatenate(
        [
            label - group * CLU_DEV + 1,
            order % BASE,
            (order // BASE) % BASE,
            order // (BASE * BASE),
            group,
            zero,
            zero,
            zero,
        ],
        axis=0,
    ).astype(jnp.float32)
    columns = table.T
    group_column = columns[:, 4:5]
    group_row = group.astype(jnp.float32)
    earlier = lax.broadcasted_iota(jnp.int32, (rows, rows), 0) < lax.broadcasted_iota(
        jnp.int32, (rows, rows), 1
    )
    rank = jnp.sum(
        jnp.where((group_column == group_row) & earlier, 1.0, 0.0), axis=0, keepdims=True
    )
    place = group * CAP + rank.astype(jnp.int32)
    place_ref[...] = place

    total = count * CAP
    chosen = jnp.where(
        lax.broadcasted_iota(jnp.int32, (total, rows), 0) == place, 1.0, 0.0
    ).astype(jnp.bfloat16)
    meta = jnp.concatenate(
        [columns, jnp.zeros((rows, LANES - columns.shape[1]), jnp.float32)], axis=1
    ).astype(jnp.bfloat16)
    copies[2].wait()
    values = emb_ref[...].astype(jnp.float32)
    scale = lax.rsqrt(jnp.sum(values * values, axis=1, keepdims=True) / features + 1e-06)
    unit = (values * scale).astype(jnp.bfloat16)
    wide = 2 * LANES
    for begin in range(0, features + LANES, wide):
        part = meta if begin == features else unit[:, begin : begin + wide]
        made = jnp.dot(chosen, part, preferred_element_type=jnp.float32)
        made = made.astype(jnp.bfloat16)
        for offset in range(0, part.shape[1], LANES):
            slots_ref[:, (begin + offset) // LANES] = made[:, offset : offset + LANES].reshape(
                count, CAP, LANES
            )


def digit_weights(shape, axis, span):
    digit = lax.broadcasted_iota(jnp.int32, shape, axis)
    start = jnp.where(digit == 0, float(span), 0.0)
    within = jnp.where(digit == 1, 1.0, jnp.where(digit == 2, float(BASE), 0.0))
    key = start + jnp.where(digit == 3, float(BASE * BASE), within)
    return start.astype(jnp.bfloat16), key.astype(jnp.bfloat16)


def nearest_earlier(span, helpers, got_ref, out_ref, rows_ref, best_ref):
    count, blocks = got_ref.shape[:2]
    total = count * CAP
    features = (blocks - 1) * LANES
    step = 512
    none = -3.0 * features
    meta = got_ref[:, blocks - 1].reshape(total, LANES)
    column_weights = digit_weights((LANES, LANES), 0, span)
    row_weights = digit_weights((8, LANES), 1, span)
    start_column, key_column = (
        jnp.dot(meta, weights, preferred_element_type=jnp.float32) for weights in column_weights
    )
    start_row, key_row = (
        lax.dot_general(
            weights, meta, (((1,), (1,)), ((), ())), preferred_element_type=jnp.float32
        )[:1, :]
        for weights in row_weights
    )
    crossed = []
    for begin in range(0, total, step):
        here = slice(begin, begin + step)
        for block in range(blocks - 1):
            rows_ref[here, block * LANES : (block + 1) * LANES] = got_ref[
                begin // CAP : (begin + step) // CAP, block
            ].reshape(step, LANES)
        column_best = jnp.full((8, step), none, jnp.float32)
        for other in range(0, begin + step, step):
            part = slice(other, other + step)
            scores = lax.dot_general(
                rows_ref[part, :],
                rows_ref[here, :],
                (((1,), (1,)), ((), ())),
                preferred_element_type=jnp.float32,
            )
            if other < begin:
                best = best_ref[part, :]
            else:
                best = jnp.full((step, LANES), none, jnp.float32)
            for lane in range(0, step, LANES):
                keys = key_row[:, begin + lane : begin + lane + LANES]
                keep = (keys >= start_column[part]) & (keys < key_column[part])
                best = jnp.where(keep, jnp.maximum(best, scores[:, lane : lane + LANES]), best)
            best_ref[part, :] = best
            if other < begin:
                keys = jnp.concatenate([key_column[part]] * (step // LANES), axis=1)
                keep = (keys >= start_row[:, here]) & (keys < key_row[:, here])
                kept = jnp.where(keep, scores, none)
                column_best = jnp.maximum(
                    column_best, jnp.max(kept.reshape(step // 8, 8, step), axis=0)
                )
        crossed.append(column_best)
    for begin in range(0, total, step):
        part = slice(begin, begin + step)
        best = best_ref[part, :]
        if begin:
            best = jnp.maximum(
                best, jnp.concatenate([crossed[begin // step]] * (LANES // 8), axis=0).T
            )
        best = jnp.max(best, axis=1, keepdims=True)
        best = jnp.maximum(best / features, -1.0)
        best_ref[part, :] = jnp.broadcast_to(best, (step, LANES))
    rings = out_ref.shape[0] // helpers
    near = helpers * CAP
    lane = lax.broadcasted_iota(jnp.int32, (rings, LANES), 1)
    for helper in range(helpers):
        result = jnp.zeros((rings, LANES), jnp.float32)
        for k in range(CORES * CAP):
            start = (k // CAP) * near + helper * CAP + k % CAP
            value = best_ref[pl.ds(start, rings, stride=CORES * near), :]
            result = jnp.where(lane == k, value, result)
        out_ref[helper * rings : (helper + 1) * rings, :] = result


def pick(helpers, core_ref, same_ref, cross_ref, place_ref, out_ref):
    chips = same_ref.shape[0]
    rows = place_ref.shape[1]
    core = core_ref[0]
    place = place_ref[...]
    group = place // CAP
    owner = group // helpers
    chip = (group - owner * helpers) * (chips // helpers) + owner // CORES
    slot = place % CAP
    same = owner % CORES == core
    mine = lax.broadcasted_iota(jnp.int32, (chips, rows), 0) == chip

    def column(ref, k):
        return jnp.where(core == 0, ref[:, k : k + 1], ref[:, CAP + k : CAP + k + 1])

    first = jnp.where(same, column(same_ref, 0), column(cross_ref, 0))
    second = jnp.where(same, column(same_ref, 1), column(cross_ref, 1))
    value = jnp.where(slot == 0, first, second)
    out_ref[...] = jnp.sum(jnp.where(mine, value, 0.0), axis=0)


def on_device(embeddings, labels, row_index):
    rows, features = embeddings.shape
    helpers = lax.axis_size("helper")
    chips = lax.axis_size("ring") * helpers
    devices = chips * CORES
    total = devices * CAP
    blocks = features // LANES + 1
    params = pltpu.CompilerParams(vmem_limit_bytes=24 * 2**20)
    hbm = pl.BlockSpec(memory_space=pltpu.HBM)
    slots, place = pl.pallas_call(
        build_slots,
        out_shape=(
            jax.ShapeDtypeStruct((devices, blocks, CAP, LANES), jnp.bfloat16),
            jax.ShapeDtypeStruct((1, rows), jnp.int32),
        ),
        in_specs=[hbm, hbm, hbm],
        scratch_shapes=[
            pltpu.VMEM((rows, features), jnp.bfloat16),
            pltpu.VMEM((rows,), jnp.int32),
            pltpu.VMEM((rows,), jnp.int32),
            pltpu.SemaphoreType.DMA((3,)),
        ],
        compiler_params=params,
        name="build_slots",
    )(*(pltpu.with_memory_space_constraint(x, pltpu.HBM) for x in (embeddings, labels, row_index)))
    got = lax.all_to_all(slots, ALL, split_axis=0, concat_axis=0, tiled=True)
    nearest = pl.pallas_call(
        functools.partial(nearest_earlier, rows * devices, helpers),
        out_shape=jax.ShapeDtypeStruct((chips, LANES), jnp.float32),
        scratch_shapes=[
            pltpu.VMEM((total, features), jnp.bfloat16),
            pltpu.VMEM((total, LANES), jnp.float32),
        ],
        compiler_params=params,
        name="nearest_earlier",
    )(got)
    returned = lax.all_to_all(
        nearest.reshape(chips, 1, LANES), PEERS, split_axis=0, concat_axis=0, tiled=True
    ).reshape(chips, LANES)
    crossed = lax.ppermute(returned, "core", [(k, CORES - 1 - k) for k in range(CORES)])
    vmem = pl.BlockSpec(memory_space=pltpu.VMEM)
    return pl.pallas_call(
        functools.partial(pick, helpers),
        out_shape=jax.ShapeDtypeStruct((rows,), jnp.float32),
        in_specs=[pl.BlockSpec(memory_space=pltpu.SMEM), vmem, vmem, vmem],
        compiler_params=params,
        name="pick",
    )(lax.axis_index("core").astype(jnp.int32).reshape(1), returned, crossed, place)


def solution(mesh):
    owners, helpers = mesh.devices.shape
    chips = jax.sharding.Mesh(
        mesh.devices.reshape(owners // CORES, CORES, helpers), ("ring", "core", "helper")
    )
    split = ("ring", "core", "helper")
    return jax.shard_map(
        on_device,
        mesh=chips,
        in_specs=(P(split, None), P(split), P(split)),
        out_specs=P(split),
        check_vma=False,
    )
```

```python
import functools

import jax
import jax.numpy as jnp
from jax import lax
from jax.experimental import pallas as pl
from jax.experimental.pallas import tpu as pltpu
from jax.sharding import PartitionSpec as P

CLU_DEV = 64
CAP = 2
LANES = 128
BASE = 64
AXES = ("owner", "helper")


def build_slots(
    emb_hbm, label_hbm, index_hbm, slots_ref, place_ref, emb_ref, label_ref, index_ref, sems
):
    rows, features = emb_ref.shape
    count = slots_ref.shape[0]
    half = rows // 2
    copies = [
        pltpu.make_async_copy(label_hbm, label_ref, sems.at[0]),
        pltpu.make_async_copy(index_hbm, index_ref, sems.at[1]),
        pltpu.make_async_copy(emb_hbm.at[:half], emb_ref.at[:half], sems.at[2]),
        pltpu.make_async_copy(emb_hbm.at[half:], emb_ref.at[half:], sems.at[3]),
    ]
    for copy in copies:
        copy.start()
    copies[0].wait()
    copies[1].wait()
    label = label_ref[...].reshape(1, rows)
    order = index_ref[...].reshape(1, rows)
    group = label // CLU_DEV
    zero = jnp.zeros_like(label)
    table = jnp.concatenate(
        [
            label - group * CLU_DEV + 1,
            order % BASE,
            (order // BASE) % BASE,
            order // (BASE * BASE),
            group,
            zero,
            zero,
            zero,
        ],
        axis=0,
    ).astype(jnp.float32)
    columns = table.T
    group_column = columns[:, 4:5]
    group_row = group.astype(jnp.float32)
    earlier = lax.broadcasted_iota(jnp.int32, (rows, rows), 0) < lax.broadcasted_iota(
        jnp.int32, (rows, rows), 1
    )
    rank = jnp.sum(
        jnp.where((group_column == group_row) & earlier, 1.0, 0.0), axis=0, keepdims=True
    )
    place = group * CAP + rank.astype(jnp.int32)
    place_ref[...] = place

    total = count * CAP
    chosen = jnp.where(
        lax.broadcasted_iota(jnp.int32, (total, rows), 0) == place, 1.0, 0.0
    ).astype(jnp.bfloat16)
    meta = jnp.concatenate(
        [columns, jnp.zeros((rows, LANES - columns.shape[1]), jnp.float32)], axis=1
    ).astype(jnp.bfloat16)
    parts = []
    for part in range(2):
        copies[2 + part].wait()
        values = emb_ref[part * half : (part + 1) * half, :].astype(jnp.float32)
        mean = jnp.sum(values * values, axis=1, keepdims=True) / features
        parts.append((values * lax.rsqrt(mean + 1e-06)).astype(jnp.bfloat16))
    unit = jnp.concatenate(parts, axis=0)
    wide = 2 * LANES
    for begin in range(0, features + LANES, wide):
        part = meta if begin == features else unit[:, begin : begin + wide]
        made = jnp.dot(chosen, part, preferred_element_type=jnp.float32)
        made = made.astype(jnp.bfloat16)
        for offset in range(0, part.shape[1], LANES):
            slots_ref[:, (begin + offset) // LANES] = made[:, offset : offset + LANES].reshape(
                count, CAP, LANES
            )


def digit_weights(shape, axis, span):
    digit = lax.broadcasted_iota(jnp.int32, shape, axis)
    start = jnp.where(digit == 0, float(span), 0.0)
    within = jnp.where(digit == 1, 1.0, jnp.where(digit == 2, float(BASE), 0.0))
    key = start + jnp.where(digit == 3, float(BASE * BASE), within)
    return start.astype(jnp.bfloat16), key.astype(jnp.bfloat16)


def nearest_earlier(span, got_ref, out_ref, rows_ref, best_ref):
    count, blocks = got_ref.shape[:2]
    total = count * CAP
    features = (blocks - 1) * LANES
    step = 512
    none = -3.0 * features
    meta = got_ref[:, blocks - 1].reshape(total, LANES)
    column_weights = digit_weights((LANES, LANES), 0, span)
    row_weights = digit_weights((8, LANES), 1, span)
    start_column, key_column = (
        jnp.dot(meta, weights, preferred_element_type=jnp.float32) for weights in column_weights
    )
    start_row, key_row = (
        lax.dot_general(
            weights, meta, (((1,), (1,)), ((), ())), preferred_element_type=jnp.float32
        )[:1, :]
        for weights in row_weights
    )
    crossed = []
    for begin in range(0, total, step):
        here = slice(begin, begin + step)
        for block in range(blocks - 1):
            rows_ref[here, block * LANES : (block + 1) * LANES] = got_ref[
                begin // CAP : (begin + step) // CAP, block
            ].reshape(step, LANES)
        column_best = jnp.full((8, step), none, jnp.float32)
        for other in range(0, begin + step, step):
            part = slice(other, other + step)
            scores = lax.dot_general(
                rows_ref[part, :],
                rows_ref[here, :],
                (((1,), (1,)), ((), ())),
                preferred_element_type=jnp.float32,
            )
            if other < begin:
                best = best_ref[part, :]
            else:
                best = jnp.full((step, LANES), none, jnp.float32)
            for lane in range(0, step, LANES):
                keys = key_row[:, begin + lane : begin + lane + LANES]
                keep = (keys >= start_column[part]) & (keys < key_column[part])
                best = jnp.where(keep, jnp.maximum(best, scores[:, lane : lane + LANES]), best)
            best_ref[part, :] = best
            if other < begin:
                keys = jnp.concatenate([key_column[part]] * (step // LANES), axis=1)
                keep = (keys >= start_row[:, here]) & (keys < key_row[:, here])
                kept = jnp.where(keep, scores, none)
                column_best = jnp.maximum(
                    column_best, jnp.max(kept.reshape(step // 8, 8, step), axis=0)
                )
        crossed.append(column_best)
    for begin in range(0, total, step):
        part = slice(begin, begin + step)
        best = best_ref[part, :]
        if begin:
            best = jnp.maximum(
                best, jnp.concatenate([crossed[begin // step]] * (LANES // 8), axis=0).T
            )
        best = jnp.max(best, axis=1, keepdims=True)
        best = jnp.maximum(best / features, -1.0)
        best_ref[part, :] = jnp.broadcast_to(best, (step, LANES))
    first = best_ref[pl.ds(0, count, stride=CAP), :]
    second = best_ref[pl.ds(1, count, stride=CAP), :]
    lane = lax.broadcasted_iota(jnp.int32, first.shape, 1)
    out_ref[...] = jnp.where(lane == 0, first, second)


def pick(returned_ref, place_ref, out_ref):
    count = returned_ref.shape[0]
    rows = place_ref.shape[1]
    place = place_ref[...]
    group = place // CAP
    second = (place - group * CAP) > 0
    value = jnp.where(second, returned_ref[:, 1:2], returned_ref[:, 0:1])
    mine = lax.broadcasted_iota(jnp.int32, (count, rows), 0) == group
    out_ref[...] = jnp.sum(jnp.where(mine, value, 0.0), axis=0)


def on_device(embeddings, labels, row_index):
    rows, features = embeddings.shape
    devices = lax.axis_size("owner") * lax.axis_size("helper")
    total = devices * CAP
    blocks = features // LANES + 1
    params = pltpu.CompilerParams(vmem_limit_bytes=24 * 2**20)
    hbm = pl.BlockSpec(memory_space=pltpu.HBM)
    slots, place = pl.pallas_call(
        build_slots,
        out_shape=(
            jax.ShapeDtypeStruct((devices, blocks, CAP, LANES), jnp.bfloat16),
            jax.ShapeDtypeStruct((1, rows), jnp.int32),
        ),
        in_specs=[hbm, hbm, hbm],
        scratch_shapes=[
            pltpu.VMEM((rows, features), jnp.bfloat16),
            pltpu.VMEM((rows,), jnp.int32),
            pltpu.VMEM((rows,), jnp.int32),
            pltpu.SemaphoreType.DMA((4,)),
        ],
        compiler_params=params,
        name="build_slots",
    )(*(pltpu.with_memory_space_constraint(x, pltpu.HBM) for x in (embeddings, labels, row_index)))
    got = lax.all_to_all(slots, AXES, split_axis=0, concat_axis=0, tiled=True)
    nearest = pl.pallas_call(
        functools.partial(nearest_earlier, rows * devices),
        out_shape=jax.ShapeDtypeStruct((devices, LANES), jnp.float32),
        scratch_shapes=[
            pltpu.VMEM((total, features), jnp.bfloat16),
            pltpu.VMEM((total, LANES), jnp.float32),
        ],
        compiler_params=params,
        name="nearest_earlier",
    )(got)
    returned = lax.all_to_all(
        nearest.reshape(devices, 1, LANES), AXES, split_axis=0, concat_axis=0, tiled=True
    )
    return pl.pallas_call(
        pick,
        out_shape=jax.ShapeDtypeStruct((rows,), jnp.float32),
        compiler_params=params,
        name="pick",
    )(returned.reshape(devices, LANES), place)


def solution(mesh):
    in_specs = (P(AXES, None), P(AXES), P(AXES))
    return jax.shard_map(
        on_device, mesh=mesh, in_specs=in_specs, out_specs=P(AXES), check_vma=False
    )
```
